256 devices in a mesh: blocks: 64 (over x_lo, y, z), filt: 4 (over x_hi, core).
Axes of the slice: x: 4 (x_hi: 2, x_lo: 2; x = x_hi * 2 + x_lo), y: 4, z: 8, core: 2. Of those that a mesh axis runs over, the one named last changes fastest.
Arguments:
- volume: bfloat16 [64, 4, 512, 128], P(None, None, 'blocks'), may hold values from -6 to 6
- w_first: bfloat16 [3, 3, 64, 64], P(None, None, 'filt'), may hold values from -0.25 to 0.25
- w_second: bfloat16 [3, 3, 3, 64, 64], P(None, None, None, 'filt'), may hold values from -0.15625 to 0.15625
- cotangent: bfloat16 [64, 4, 512, 128], P('filt', None, 'blocks'), may hold values from -6 to 6
Outputs:
- output: bfloat16 [64, 4, 512, 128], P('filt', None, 'blocks')
- input_grad: bfloat16 [64, 4, 512, 128], P('filt', None, 'blocks')
- first_grad: float32 [3, 3, 64, 64], P(None, None, 'filt')
- second_grad: float32 [3, 3, 3, 64, 64], P(None, None, None, 'filt')
The draws below stay inside these ranges and needn't reach their ends.
All inputs are finite; a program needn't handle non-finite values.
Results may differ from the reference program's by a relative error of at most 0.012.
Values may be sent and summed in bfloat16 or wider, within the bound.
No kernel may reach another device: no remote copies, remote signals or barrier semaphores. Data moves between devices by JAX's collectives and lax.ppermute only.
A program may use at most 64 MiB of HBM per device.

```python
import math
import jax
import jax.numpy as jnp
from jax import lax

C = 64
Z = 4
X = 128
NY = 512


def block_scale(key, shape, cuts, least, top_value):
    def one(axis_at, parts):
        draws = jax.random.uniform(jax.random.fold_in(jax.random.fold_in(key, 6), axis_at), (parts,), jnp.float32, least / len(cuts), top_value / len(cuts))
        return jnp.repeat(jnp.exp(draws), shape[axis_at] // parts).reshape((-1,) + (1,) * (len(shape) - axis_at - 1))

    factor_of = one(*cuts[0])
    for cut in cuts[1:]:
        factor_of = factor_of * one(*cut)
    return factor_of


def noise(own_key, dims, width, reach, shards=(), kind=jnp.bfloat16):
    loudness = block_scale(own_key, dims, shards, -0.22, 0.18) if shards else 1.0
    drawn = jax.random.normal(own_key, dims, jnp.float32) * width * loudness
    return jnp.minimum(jnp.maximum(drawn, -reach), reach).astype(kind)


def setup_inputs(seed: int = 0) -> dict:
    arg_keys = jax.random.split(jax.random.key(seed), 5)
    volume = noise(arg_keys[0], (C, Z, NY, X), 1.0, 6.0, ((2, 64),))
    w_first = noise(arg_keys[1], (3, 3, C, C), (9 * C) ** -0.5, 0.25, ((2, 4),))
    w_second = noise(arg_keys[2], (3, 3, 3, C, C), (27 * C) ** -0.5, 0.15625, ((3, 4),))
    cotangent = noise(arg_keys[3], (C, Z, NY, X), 1.0, 6.0, ((0, 4), (2, 64)))
    return dict(volume=volume, w_first=w_first, w_second=w_second, cotangent=cotangent)


def convolve(field, kernel, dilation, padding):
    result = lax.conv_general_dilated(field[None], kernel, (1, 1, 1), padding, rhs_dilation=dilation, dimension_numbers=('NCDHW', 'DHWOI', 'NCDHW'))
    return result[0]

def first_layer(field, kernel):
    return convolve(field, kernel, (1, 1, 1), ((0, 0), (1, 1), (1, 1)))

def second_layer(field, kernel):
    return convolve(field, kernel, (2, 2, 2), ((2, 2), (2, 2), (2, 2)))

def reference(volume, w_first, w_second, cotangent):
    source = volume.astype(jnp.float32)
    kernel_one = w_first.astype(jnp.float32)[None]
    kernel_two = w_second.astype(jnp.float32)
    pre = first_layer(source, kernel_one)
    hidden = jax.nn.silu(pre).astype(jnp.bfloat16)
    result, pull_two = jax.vjp(second_layer, hidden.astype(jnp.float32), kernel_two)
    output = result.astype(jnp.bfloat16)
    hidden_grad, second_raw = pull_two(cotangent.astype(jnp.float32))
    sigma = jax.nn.sigmoid(pre)
    pre_grad = (hidden_grad * sigma * (1.0 + pre * (1.0 - sigma))).astype(jnp.bfloat16)
    unused, pull_one = jax.vjp(first_layer, source, kernel_one)
    input_raw, first_raw = pull_one(pre_grad.astype(jnp.float32))
    factor = 1.0 / math.sqrt(Z * NY * X)
    return (output, input_raw.astype(jnp.bfloat16), first_raw[0] * factor, second_raw * factor)
```

```python
import jax
import jax.numpy as jnp
from jax import lax
from jax.experimental import pallas as pl
from jax.experimental.pallas import tpu as pltpu
from jax.sharding import Mesh, PartitionSpec as P

BLOCKS = ("x_lo", "y", "z")
FILT = ("x_hi", "core")
SPLIT = {"x_lo": 2, "y": 4, "z": 8, "x_hi": 2, "core": 2}
BF = jnp.bfloat16
F32 = jnp.float32
SWAP = [(0, 1), (1, 0)]


def dot(left, right):
    return lax.dot_general(left, right, (((1,), (0,)), ((), ())), preferred_element_type=F32)


def dot_cells(left, right):
    return lax.dot_general(left, right, (((1,), (1,)), ((), ())), preferred_element_type=F32)


def shifted(value, amount):
    lane = lax.broadcasted_iota(jnp.int32, value.shape, 1)
    width = value.shape[1]
    moved = pltpu.roll(value, amount % width, 1)
    inside = lane >= amount if amount > 0 else lane < width + amount
    return jnp.where(inside, moved, 0.0)


def forward_kernel(place, vol, vol_lo, vol_hi, w1, w2, cot, out, slope, grads, hidden):
    def row(z, y):
        if y < 0:
            return vol_lo[z, y + 3]
        return vol_hi[z, y - 8] if y >= 8 else vol[z, y]

    weights = w1[...]
    for z in range(4):
        for base in range(-2, 10, 4):
            ys = range(base, base + 4)
            cells = jnp.concatenate(
                [jnp.concatenate([row(z, y - 1), row(z, y), row(z, y + 1)], 0) for y in ys], 1
            )
            product = dot(weights, cells)
            for n, y in enumerate(ys):
                part = product[:, n * 128 : n * 128 + 128]
                pre = shifted(part[:64], 1) + part[64:128] + shifted(part[128:], -1)
                sigma = 1.0 / (1.0 + jnp.exp(-pre))
                value = pre * sigma
                if y < 0:
                    value = jnp.where(place[0] > 0, 0.0, value)
                if y >= 8:
                    value = jnp.where(place[1] > 0, 0.0, value)
                hidden[z, y + 2] = value.astype(BF)
                if -1 <= y <= 8:
                    slope[z, y + 1] = sigma * (1.0 + pre * (1.0 - sigma))
    weights = w2[...]
    total = None
    for p in range(2):
        for base in range(0, 8, 4):
            ys = range(base, base + 4)
            cells = jnp.concatenate(
                [
                    jnp.concatenate(
                        [hidden[p + 2 * q, y + 2 * b] for q in range(2) for b in range(3)], 0
                    )
                    for y in ys
                ],
                1,
            )
            product = dot(weights, cells)
            for n, y in enumerate(ys):
                part = product[:, n * 128 : n * 128 + 128]
                for q in range(2):
                    k = 48 * q
                    value = (
                        shifted(part[k : k + 16], 2)
                        + part[k + 16 : k + 32]
                        + shifted(part[k + 32 : k + 48], -2)
                    )
                    out[p + 2 * q, y] = value.astype(BF)
            left = []
            for y in ys:
                pieces = []
                for q in range(2):
                    own = cot[p + 2 * q, y]
                    wide = own.astype(F32)
                    pieces += [shifted(wide, -2).astype(BF), own, shifted(wide, 2).astype(BF)]
                left.append(jnp.concatenate(pieces, 0))
            term = dot_cells(jnp.concatenate(left, 1), cells)
            total = term if total is None else total + term
    grads[...] = total


def backward_kernel(
    place, cot, cot_lo, cot_hi, slope, vol, vol_lo, vol_hi, w1, w2, second, out, packed, pre_grad
):
    def grad_row(r, z, y):
        if y < 0:
            return cot_lo[r, z, y + 3]
        return cot_hi[r, z, y - 8] if y >= 8 else cot[r, z, y]

    def row(z, y):
        if y < 0:
            return vol_lo[z, y + 3]
        return vol_hi[z, y - 8] if y >= 8 else vol[z, y]

    weights = w2[...]
    for p in range(2):
        for base in range(-1, 9, 2):
            ys = range(base, base + 2)
            cells = jnp.concatenate(
                [
                    jnp.concatenate(
                        [
                            grad_row(r, p + 2 * q, y - 2 * (b - 1))
                            for q in range(2)
                            for b in range(3)
                            for r in range(4)
                        ],
                        0,
                    )
                    for y in ys
                ],
                1,
            )
            product = dot(weights, cells)
            for n, y in enumerate(ys):
                part = product[:, n * 128 : n * 128 + 128]
                for q in range(2):
                    k = 192 * q
                    value = (
                        shifted(part[k : k + 64], -2)
                        + part[k + 64 : k + 128]
                        + shifted(part[k + 128 : k + 192], 2)
                    )
                    value = value * slope[p + 2 * q, y + 1]
                    if y < 0:
                        value = jnp.where(place[0] > 0, 0.0, value)
                    if y >= 8:
                        value = jnp.where(place[1] > 0, 0.0, value)
                    pre_grad[p + 2 * q, y + 1] = value.astype(BF)
    weights = w1[...]
    mine = pl.multiple_of(place[2] * 16, 16)
    total = None
    for z in range(4):
        for base in range(0, 8, 4):
            ys = range(base, base + 4)
            cells = jnp.concatenate(
                [
                    jnp.concatenate([pre_grad[z, y + 1 - (b - 1)] for b in range(3)], 0)
                    for y in ys
                ],
                1,
            )
            product = dot(weights, cells)
            for n, y in enumerate(ys):
                part = product[:, n * 128 : n * 128 + 128]
                value = shifted(part[:16], -1) + part[16:32] + shifted(part[32:48], 1)
                out[z, y] = value.astype(BF)
            left = []
            for y in ys:
                own = pre_grad[z, y + 1, pl.ds(mine, 16), :]
                wide = own.astype(F32)
                left.append(
                    jnp.concatenate([shifted(wide, -1).astype(BF), own, shifted(wide, 1).astype(BF)], 0)
                )
            source = jnp.concatenate(
                [jnp.concatenate([row(z, y - 1), row(z, y), row(z, y + 1)], 0) for y in ys], 1
            )
            term = dot_cells(jnp.concatenate(left, 1), source)
            total = term if total is None else total + term
    raw = second[...]
    rows = jnp.concatenate(
        [
            raw[48:, :192],
            raw[:48, :192] + raw[48:, 192:],
            raw[:48, 192:],
            total,
        ],
        0,
    ) * (1.0 / 512.0)
    for k in range(24):
        packed[k] = rows[8 * k : 8 * k + 8, :128]
    for k in range(12):
        packed[24 + k] = jnp.concatenate(
            [rows[8 * k : 8 * k + 8, 128:], rows[96 + 8 * k : 104 + 8 * k, 128:]], 1
        )
    packed[36:] = jnp.zeros((28, 8, 128), F32)


def spread_kernel(tiles, first, second):
    for g in range(4):
        for c in range(3):
            for half in range(2):
                t = g * 6 + c * 2 + half
                main = tiles[t]
                rest = tiles[24 + t % 12]
                parts = [main[:, :64], main[:, 64:], rest[:, :64] if t < 12 else rest[:, 64:]]
                for b in range(3):
                    if g < 3:
                        second[g, b, c, 8 * half : 8 * half + 8, :] = parts[b]
                    else:
                        first[b, c, 8 * half : 8 * half + 8, :] = parts[b]


SMEM = pl.BlockSpec(memory_space=pltpu.SMEM)
VMEM = pl.BlockSpec(memory_space=pltpu.VMEM)


def call(kernel, operands, outs, scratch=(), scalars=True):
    specs = [SMEM] + [VMEM] * (len(operands) - 1) if scalars else [VMEM] * len(operands)
    return pl.pallas_call(
        kernel,
        in_specs=specs,
        out_specs=tuple(VMEM for _ in outs),
        out_shape=tuple(jax.ShapeDtypeStruct(shape, kind) for shape, kind in outs),
        scratch_shapes=list(scratch),
    )(*operands)


def neighbours(rows):
    count = 64
    forward = [(i, i + 1) for i in range(count - 1)]
    backward = [(i + 1, i) for i in range(count - 1)]
    return (
        lax.ppermute(rows[..., 5:8, :, :], BLOCKS, forward),
        lax.ppermute(rows[..., 0:3, :, :], BLOCKS, backward),
    )


def per_device(volume, w_first, w_second, cotangent):
    block = lax.axis_index(BLOCKS)
    mine = lax.axis_index(FILT)
    place = jnp.stack([block == 0, block == 63, mine]).astype(jnp.int32)
    vol = volume.transpose(1, 2, 0, 3)
    vol_lo, vol_hi = neighbours(vol)
    cot = cotangent.transpose(1, 2, 0, 3)
    kernels = jnp.concatenate([w_first.reshape(9, 16, 64), w_second.reshape(27, 16, 64)], 0)
    bundle = jnp.concatenate(
        [cot.reshape(32, 16, 128), jnp.concatenate([kernels[:18], kernels[18:]], 2)], 0
    )[None]
    bundle = jnp.concatenate([bundle, lax.ppermute(bundle, "x_hi", SWAP)], 0)
    bundle = jnp.concatenate([bundle, lax.ppermute(bundle, "core", SWAP)], 0)
    cot_all = bundle[:, :32].reshape(4, 4, 8, 16, 128)
    cot_lo, cot_hi = neighbours(cot_all)
    kernels = jnp.concatenate([bundle[:, 32:, :, :64], bundle[:, 32:, :, 64:]], 1)
    places = [((f ^ mine) & 1) * 2 + ((f ^ mine) >> 1) for f in range(4)]
    ordered = jnp.stack(
        [lax.dynamic_index_in_dim(kernels[:, :9], at, 0, False) for at in places]
    )
    full_first = ordered.reshape(4, 3, 3, 16, 64)
    w1_forward = full_first.transpose(2, 0, 3, 1, 4).reshape(192, 192)
    own_inputs = lax.dynamic_slice_in_dim(full_first, mine * 16, 16, 4)
    w1_backward = own_inputs.transpose(2, 4, 1, 0, 3).reshape(48, 192)
    w2_forward = (
        jnp.stack([jnp.stack([w_second[1 + q - z] for q in range(2)]) for z in range(2)])
        .transpose(0, 3, 4, 1, 2, 5)
        .reshape(96, 384)
    )
    full_second = kernels[:, 9:].reshape(4, 3, 3, 3, 16, 64)
    w2_backward = (
        jnp.stack([jnp.stack([full_second[:, 1 + z - q] for q in range(2)]) for z in range(2)])
        .transpose(0, 4, 6, 1, 3, 2, 5)
        .reshape(384, 384)
    )
    output, slope, second = call(
        forward_kernel,
        (place, vol, vol_lo, vol_hi, w1_forward, w2_forward, cot),
        (((4, 8, 16, 128), BF), ((4, 10, 64, 128), F32), ((96, 384), F32)),
        [pltpu.VMEM((4, 12, 64, 128), BF)],
    )
    input_grad, packed = call(
        backward_kernel,
        (place, cot_all, cot_lo, cot_hi, slope, vol, vol_lo, vol_hi, w1_backward, w2_backward, second),
        (((4, 8, 16, 128), BF), ((64, 8, 128), F32)),
        [pltpu.VMEM((4, 10, 64, 128), BF)],
    )
    shares = lax.all_to_all(packed, BLOCKS, 0, 0)
    summed = jnp.broadcast_to(jnp.sum(shares, 0)[None], (64, 8, 128))
    tiles = lax.all_to_all(summed, BLOCKS, 0, 0)
    first_grad, second_grad = call(
        spread_kernel,
        (tiles,),
        (((3, 3, 16, 64), F32), ((3, 3, 3, 16, 64), F32)),
        scalars=False,
    )
    return (output.transpose(2, 0, 1, 3), input_grad.transpose(2, 0, 1, 3), first_grad, second_grad)


def solution(mesh):
    fine = Mesh(mesh.devices.reshape(tuple(SPLIT.values())), tuple(SPLIT))
    return jax.shard_map(
        per_device,
        mesh=fine,
        in_specs=(
            P(None, None, BLOCKS, None),
            P(None, None, FILT, None),
            P(None, None, None, FILT, None),
            P(FILT, None, BLOCKS, None),
        ),
        out_specs=(
            P(FILT, None, BLOCKS, None),
            P(FILT, None, BLOCKS, None),
            P(None, None, FILT, None),
            P(None, None, None, FILT, None),
        ),
        check_vma=False,
    )
```

```python
import jax
import jax.numpy as jnp
from jax import lax
from jax.experimental import pallas as pl
from jax.experimental.pallas import tpu as pltpu
from jax.sharding import Mesh, PartitionSpec as P


BLOCKS = ("x_lo", "y", "z")
FILT = ("x_hi", "core")
SPLIT = {"x_lo": 2, "y": 4, "z": 8, "x_hi": 2, "core": 2}
BF = jnp.bfloat16
F32 = jnp.float32
SWAP = [(0, 1), (1, 0)]


def dot(left, right):
    return lax.dot_general(left, right, (((1,), (0,)), ((), ())), preferred_element_type=F32)


def dot_cells(left, right):
    return lax.dot_general(left, right, (((1,), (1,)), ((), ())), preferred_element_type=F32)


def shifted(value, amount):
    lane = lax.broadcasted_iota(jnp.int32, value.shape, 1)
    width = value.shape[1]
    moved = pltpu.roll(value, amount % width, 1)
    inside = lane >= amount if amount > 0 else lane < width + amount
    return jnp.where(inside, moved, 0.0)


def prepare_kernel(volume, cotangent, w_first, w_second, vol, down, up, grads, kernels, own):
    for z in range(4):
        rows = jnp.swapaxes(volume[:, z].astype(F32), 0, 1).astype(BF)
        vol[z] = rows
        mine = jnp.swapaxes(cotangent[:, z].astype(F32), 0, 1).astype(BF)
        grads[8 * z : 8 * z + 8] = mine
        own[8 * z : 8 * z + 8] = mine
        for n in range(3):
            k = 3 * z + n
            down[k] = mine[5 + n]
            up[k] = mine[n]
            down[12 + 4 * k : 16 + 4 * k] = rows[5 + n].reshape(4, 16, 128)
            up[12 + 4 * k : 16 + 4 * k] = rows[n].reshape(4, 16, 128)
    strips = [w_first[b, c] for c in range(3) for b in range(3)]
    strips += [w_second[a, b, c] for a in range(3) for b in range(3) for c in range(3)]
    for n in range(18):
        pair = jnp.concatenate(strips[2 * n : 2 * n + 2], 1)
        kernels[n] = pair
        own[32 + n] = pair


def strip(kernels, base, n):
    k = base + 3 * (n // 2)
    if n % 2 == 0:
        return jnp.concatenate([kernels[k], kernels[k + 1][:, :64]], 1)
    return jnp.concatenate([kernels[k + 1][:, 64:], kernels[k + 2]], 1)


def volume_row(vol, low, high, z, y):
    if 0 <= y < 8:
        return vol[z, y]
    source, n = (low, y + 3) if y < 0 else (high, y - 8)
    k = 12 + 4 * (3 * z + n)
    return source[k : k + 4].reshape(64, 128)


def stacked_rows(vol, low, high, z, y):
    return jnp.concatenate([volume_row(vol, low, high, z, y + n) for n in (-1, 0, 1)], 0)


def build_first(spot, kernels, w1_full):
    for r in range(4):
        f = pl.multiple_of((spot ^ r) * 16, 16)
        for c in range(3):
            w1_full[c, pl.ds(f, 16), :] = strip(*kernels[r], c)


def forward_kernel(
    place,
    vol,
    low,
    high,
    part0,
    kernels0,
    kernels1,
    kernels2,
    kernels3,
    hidden,
    slope,
    grads,
    w2_turned,
    w1_full,
):
    kernels = ((kernels0, 0), (kernels1, 32), (kernels2, 0), (kernels3, 0))
    build_first(place[2], kernels, w1_full)

    turned = jnp.concatenate(
        [
            jnp.concatenate([strip(*kernels[r], 3 + 3 * (1 + z - q) + b) for z in range(2)], 1)
            for q in range(2)
            for b in range(3)
            for r in range(4)
        ],
        0,
    )
    w2_turned[...] = turned.T.reshape(6, 64, 384)
    weights = w1_full[...].reshape(192, 192)
    for z in range(4):
        for base in range(-2, 10, 4):
            ys = range(base, base + 4)
            cells = jnp.concatenate([stacked_rows(vol, low, high, z, y) for y in ys], 1)
            product = dot(weights, cells)
            for n, y in enumerate(ys):
                part = product[:, n * 128 : n * 128 + 128]
                pre = shifted(part[:64], 1) + part[64:128] + shifted(part[128:], -1)
                sigma = 1.0 / (1.0 + jnp.exp(-pre))
                value = pre * sigma
                if y < 0:
                    value = jnp.where(place[0] > 0, 0.0, value)
                if y >= 8:
                    value = jnp.where(place[1] > 0, 0.0, value)
                hidden[z, y + 2] = value.astype(BF)
                if -1 <= y <= 8:
                    slope[z, y + 1] = sigma * (1.0 + pre * (1.0 - sigma))
    total = None
    for p in range(2):
        for base in range(0, 8, 4):
            ys = range(base, base + 4)
            left = []
            for y in ys:
                pieces = []
                for q in range(2):
                    own = part0[8 * (p + 2 * q) + y]
                    wide = own.astype(F32)
                    pieces += [shifted(wide, -2).astype(BF), own, shifted(wide, 2).astype(BF)]
                left.append(jnp.concatenate(pieces, 0))
            term = dot_cells(jnp.concatenate(left, 1), hidden_rows(hidden, p, ys))
            total = term if total is None else total + term
    grads[...] = total


def hidden_rows(hidden, p, ys):
    return jnp.concatenate(
        [
            jnp.concatenate([hidden[p + 2 * q, y + 2 * b] for q in range(2) for b in range(3)], 0)
            for y in ys
        ],
        1,
    )


def grad_rows(parts, rims, p, ys):
    def grad_row(r, z, y):
        if 0 <= y < 8:
            return parts[r][8 * z + y]
        return rims[r][3 * z + y + 3] if y < 0 else rims[r][12 + 3 * z + y - 8]

    return jnp.concatenate(
        [
            jnp.concatenate(
                [
                    grad_row(r, p + 2 * q, y - 2 * (b - 1))
                    for q in range(2)
                    for b in range(3)
                    for r in range(4)
                ],
                0,
            )
            for y in ys
        ],
        1,
    )


def first_grad_kernel(
    place,
    vol,
    low,
    high,
    part0,
    part1,
    part2,
    part3,
    rim0,
    rim1,
    rim2,
    rim3,
    slope,
    second,
    w2_turned,
    packed,
    own_grad,
):
    parts = (part0, part1, part2, part3)
    rims = (rim0, rim1, rim2, rim3)
    mine = pl.multiple_of(place[2] * 16, 16)
    weights = w2_turned[:, pl.ds(mine, 16), :].reshape(96, 384)
    for p in range(2):
        for base in range(0, 8, 4):
            ys = range(base, base + 4)
            product = dot(weights, grad_rows(parts, rims, p, ys))
            for n, y in enumerate(ys):
                part = product[:, n * 128 : n * 128 + 128]
                for q in range(2):
                    k = 48 * q
                    value = (
                        shifted(part[k : k + 16], -2)
                        + part[k + 16 : k + 32]
                        + shifted(part[k + 32 : k + 48], 2)
                    )
                    value = value * slope[p + 2 * q, y + 1, pl.ds(mine, 16), :]
                    own_grad[p + 2 * q, y] = value.astype(BF)
    total = None
    for z in range(4):
        for base in range(0, 8, 4):
            ys = range(base, base + 4)
            left = []
            for y in ys:
                own = own_grad[z, y]
                wide = own.astype(F32)
                left.append(
                    jnp.concatenate([shifted(wide, -1).astype(BF), own, shifted(wide, 1).astype(BF)], 0)
                )
            source = jnp.concatenate([stacked_rows(vol, low, high, z, y) for y in ys], 1)
            term = dot_cells(jnp.concatenate(left, 1), source)
            total = term if total is None else total + term
    raw = second[...]
    rows = jnp.concatenate(
        [raw[48:, :192], raw[:48, :192] + raw[48:, 192:], raw[:48, 192:], total], 0
    ) * (1.0 / 512.0)
    for k in range(24):
        packed[k] = rows[8 * k : 8 * k + 8, :128]
    for k in range(12):
        packed[24 + k] = jnp.concatenate(
            [rows[8 * k : 8 * k + 8, 128:], rows[96 + 8 * k : 104 + 8 * k, 128:]], 1
        )
    packed[36:] = jnp.zeros((28, 8, 128), F32)


def outputs_kernel(
    place,
    hidden,
    part0,
    part1,
    part2,
    part3,
    rim0,
    rim1,
    rim2,
    rim3,
    slope,
    kernels0,
    kernels1,
    kernels2,
    kernels3,
    w2_turned,
    out,
    input_grad,
    pre_grad,
    w1_full,
    w1_turned,
):
    kernels = ((kernels0, 0), (kernels1, 32), (kernels2, 0), (kernels3, 0))
    build_first(place[2], kernels, w1_full)
    parts = (part0, part1, part2, part3)
    rims = (rim0, rim1, rim2, rim3)
    mine = pl.multiple_of(place[2] * 16, 16)
    weights = jnp.concatenate(
        [
            jnp.concatenate(
                [
                    strip(kernels0, 0, 3 + 3 * (1 + q - z) + b)[:, 64 * c : 64 * c + 64]
                    for q in range(2)
                    for b in range(3)
                ],
                1,
            )
            for z in range(2)
            for c in range(3)
        ],
        0,
    )
    for p in range(2):
        for base in range(0, 8, 4):
            ys = range(base, base + 4)
            product = dot(weights, hidden_rows(hidden, p, ys))
            for n, y in enumerate(ys):
                part = product[:, n * 128 : n * 128 + 128]
                for q in range(2):
                    k = 48 * q
                    value = (
                        shifted(part[k : k + 16], 2)
                        + part[k + 16 : k + 32]
                        + shifted(part[k + 32 : k + 48], -2)
                    )
                    out[p + 2 * q, y] = value.astype(BF)
    weights = w2_turned[...].reshape(384, 384)
    for p in range(2):
        for base in range(-1, 9, 2):
            ys = range(base, base + 2)
            product = dot(weights, grad_rows(parts, rims, p, ys))
            for n, y in enumerate(ys):
                part = product[:, n * 128 : n * 128 + 128]
                for q in range(2):
                    k = 192 * q
                    value = (
                        shifted(part[k : k + 64], -2)
                        + part[k + 64 : k + 128]
                        + shifted(part[k + 128 : k + 192], 2)
                    )
                    value = value * slope[p + 2 * q, y + 1]
                    if y < 0:
                        value = jnp.where(place[0] > 0, 0.0, value)
                    if y >= 8:
                        value = jnp.where(place[1] > 0, 0.0, value)
                    pre_grad[p + 2 * q, y + 1] = value.astype(BF)
    for c in range(3):
        turned = w1_full[c].astype(F32).T
        w1_turned[c] = jnp.concatenate([turned[64 * b : 64 * b + 64] for b in range(3)], 1)
    weights = w1_turned[:, pl.ds(mine, 16), :].reshape(48, 192).astype(BF)
    for z in range(4):
        for base in range(0, 8, 4):
            ys = range(base, base + 4)
            cells = jnp.concatenate(
                [jnp.concatenate([pre_grad[z, y + 2 - b] for b in range(3)], 0) for y in ys], 1
            )
            product = dot(weights, cells)
            for n, y in enumerate(ys):
                part = product[:, n * 128 : n * 128 + 128]
                value = shifted(part[:16], -1) + part[16:32] + shifted(part[32:48], 1)
                input_grad[z, y] = value.astype(BF)


def sum_kernel(shares, summed):
    summed[...] = jnp.broadcast_to(jnp.sum(shares[...], 0).astype(BF)[None], (64, 8, 128))


def spread_kernel(tiles, first, second):
    for g in range(4):
        for c in range(3):
            for half in range(2):
                t = g * 6 + c * 2 + half
                main = tiles[t].astype(F32)
                rest = tiles[24 + t % 12].astype(F32)
                parts = [main[:, :64], main[:, 64:], rest[:, :64] if t < 12 else rest[:, 64:]]
                for b in range(3):
                    if g < 3:
                        second[g, b, c, 8 * half : 8 * half + 8, :] = parts[b]
                    else:
                        first[b, c, 8 * half : 8 * half + 8, :] = parts[b]


SMEM = pl.BlockSpec(memory_space=pltpu.SMEM)
VMEM = pl.BlockSpec(memory_space=pltpu.VMEM)


def call(kernel, operands, outs, scratch=(), scalars=1, source=pltpu.VMEM, near=True, far=()):
    operands = list(operands)
    for n in range(scalars, len(operands)):
        space = pltpu.HBM if n in far else source
        operands[n] = pltpu.with_memory_space_constraint(operands[n], space)
    return pl.pallas_call(
        kernel,
        in_specs=[SMEM] * scalars + [VMEM] * (len(operands) - scalars),
        out_specs=tuple(VMEM for _ in outs),
        out_shape=tuple(
            pltpu.VMEM(shape, kind) if near else jax.ShapeDtypeStruct(shape, kind)
            for shape, kind in outs
        ),
        scratch_shapes=list(scratch),
        compiler_params=pltpu.CompilerParams(vmem_limit_bytes=16 << 20),
    )(*operands)


FORWARD = [(i, i + 1) for i in range(63)]
BACKWARD = [(i + 1, i) for i in range(63)]
ACROSS = [(i, 3 - i) for i in range(4)]


def per_device(volume, w_first, w_second, cotangent):
    block = lax.axis_index(BLOCKS)
    mine = lax.axis_index(FILT)
    place = jnp.stack([block == 0, block == 63, mine]).astype(jnp.int32)
    rows = ((32, 16, 128), BF)
    taps = ((18, 16, 128), BF)
    rim = ((60, 16, 128), BF)
    vol, down, up, part0, kernels0, own = call(
        prepare_kernel,
        (volume, cotangent, w_first, w_second),
        (((4, 8, 64, 128), BF), rim, rim, rows, taps, ((50, 16, 128), BF)),
        scalars=0,
        source=pltpu.HBM,
    )
    part2 = lax.ppermute(part0, "x_hi", SWAP)
    low = lax.ppermute(down, BLOCKS, FORWARD)
    high = lax.ppermute(up, BLOCKS, BACKWARD)
    kernels2 = lax.ppermute(kernels0, ("x_lo", "x_hi"), ACROSS)
    part1 = lax.ppermute(own, "core", SWAP)
    part3 = lax.ppermute(part2, "core", SWAP)
    kernels3 = lax.ppermute(kernels2, "core", SWAP)
    rim0 = jnp.concatenate([low[:12], high[:12]], 0)
    rim2 = lax.ppermute(rim0, "x_hi", SWAP)
    rim1 = lax.ppermute(rim0, "core", SWAP)
    rim3 = lax.ppermute(rim2, "core", SWAP)
    parts = (part0, part1, part2, part3)
    kernels = (kernels0, part1, kernels2, kernels3)
    rims = (rim0, rim1, rim2, rim3)
    hidden, slope, second, w2_turned = call(
        forward_kernel,
        (place, vol, low, high, part0) + kernels,
        (
            ((4, 12, 64, 128), BF),
            ((4, 10, 64, 128), F32),
            ((96, 384), F32),
            ((6, 64, 384), BF),
        ),
        [pltpu.VMEM((3, 64, 192), BF)],
    )
    (packed,) = call(
        first_grad_kernel,
        (place, vol, low, high) + parts + rims + (slope, second, w2_turned),
        (((64, 8, 128), F32),),
        [pltpu.VMEM((4, 8, 16, 128), BF)],
    )
    shares = lax.all_to_all(packed, BLOCKS, 0, 0)
    output, input_grad = call(
        outputs_kernel,
        (place, hidden) + parts + rims + (slope,) + kernels + (w2_turned,),
        (((4, 8, 16, 128), BF), ((4, 8, 16, 128), BF)),
        [
            pltpu.VMEM((4, 10, 64, 128), BF),
            pltpu.VMEM((3, 64, 192), BF),
            pltpu.VMEM((3, 64, 192), F32),
        ],
        far=(1, 6, 7, 8, 9, 11, 13, 14),
    )
    (summed,) = call(sum_kernel, (shares,), (((64, 8, 128), BF),), scalars=0)
    tiles = lax.all_to_all(summed, BLOCKS, 0, 0)
    first_grad, second_grad = call(
        spread_kernel,
        (tiles,),
        (((3, 3, 16, 64), F32), ((3, 3, 3, 16, 64), F32)),
        scalars=0,
        near=False,
    )
    return (output.transpose(2, 0, 1, 3), input_grad.transpose(2, 0, 1, 3), first_grad, second_grad)


def solution(mesh):
    fine = Mesh(mesh.devices.reshape(tuple(SPLIT.values())), tuple(SPLIT))
    return jax.shard_map(
        per_device,
        mesh=fine,
        in_specs=(
            P(None, None, BLOCKS, None),
            P(None, None, FILT, None),
            P(None, None, None, FILT, None),
            P(FILT, None, BLOCKS, None),
        ),
        out_specs=(
            P(FILT, None, BLOCKS, None),
            P(FILT, None, BLOCKS, None),
            P(None, None, FILT, None),
            P(None, None, None, FILT, None),
        ),
        check_vma=False,
    )
```

```python
import jax
import jax.numpy as jnp
from jax import lax
from jax.experimental import pallas as pl
from jax.experimental.pallas import tpu as pltpu
from jax.sharding import Mesh, PartitionSpec as P


BLOCKS = ("x_lo", "y", "z")
FILT = ("x_hi", "core")
SPLIT = {"x_lo": 2, "y": 4, "z": 8, "x_hi": 2, "core": 2}
BF = jnp.bfloat16
F32 = jnp.float32
SWAP = [(0, 1), (1, 0)]


def dot(left, right):
    return lax.dot_general(left, right, (((1,), (0,)), ((), ())), preferred_element_type=F32)


def dot_cells(left, right):
    return lax.dot_general(left, right, (((1,), (1,)), ((), ())), preferred_element_type=F32)


def shifted(value, amount):
    lane = lax.broadcasted_iota(jnp.int32, value.shape, 1)
    width = value.shape[1]
    moved = pltpu.roll(value, amount % width, 1)
    inside = lane >= amount if amount > 0 else lane < width + amount
    return jnp.where(inside, moved, 0.0)


def prepare_kernel(volume, cotangent, w_first, w_second, vol, near, far, grads, kernels, own):
    odd = lax.axis_index("z") & 1
    for z in range(4):
        rows = jnp.swapaxes(volume[:, z].astype(F32), 0, 1).astype(BF)
        vol[z] = rows
        mine = jnp.swapaxes(cotangent[:, z].astype(F32), 0, 1).astype(BF)
        grads[8 * z : 8 * z + 8] = mine
        own[8 * z : 8 * z + 8] = mine
        for n in range(3):
            k = 3 * z + n
            for edge, start in ((near, 5 * (1 - odd)), (far, 5 * odd)):
                edge[k] = grads[8 * z + start + n]
                edge[12 + 4 * k : 16 + 4 * k] = vol[z, start + n].reshape(4, 16, 128)
    strips = [w_first[b, c] for c in range(3) for b in range(3)]
    strips += [w_second[a, b, c] for a in range(3) for b in range(3) for c in range(3)]
    for n in range(18):
        pair = jnp.concatenate(strips[2 * n : 2 * n + 2], 1)
        kernels[n] = pair
        own[32 + n] = pair


def position():
    block = lax.axis_index(BLOCKS)
    return block == 0, block == 63, lax.axis_index(FILT)


def strip(kernels, base, n):
    k = base + 3 * (n // 2)
    if n % 2 == 0:
        return jnp.concatenate([kernels[k], kernels[k + 1][:, :64]], 1)
    return jnp.concatenate([kernels[k + 1][:, 64:], kernels[k + 2]], 1)


def volume_row(vol, halo, z, y):
    if 0 <= y < 8:
        return vol[z, y]
    return halo[z, y + 3 if y < 0 else y - 5]


def stacked_rows(vol, halo, z, y):
    return jnp.concatenate([volume_row(vol, halo, z, y + n) for n in (-1, 0, 1)], 0)


def build_halo(near, far, halo):
    odd = lax.axis_index("z") & 1
    for edge, start in ((near, 3 * (1 - odd)), (far, 3 * odd)):
        for z in range(4):
            for n in range(3):
                k = 12 + 4 * (3 * z + n)
                halo[z, start + n] = edge[k : k + 4].reshape(64, 128)


def build_first(spot, kernels, w1_full):
    for r in range(4):
        f = pl.multiple_of((spot ^ r) * 16, 16)
        for c in range(3):
            w1_full[c, pl.ds(f, 16), :] = strip(*kernels[r], c)


def forward_kernel(
    vol,
    near,
    far,
    part0,
    kernels0,
    kernels1,
    kernels2,
    kernels3,
    hidden_out,
    slope,
    grads,
    w1_full,
    w2_own,
    w2_turned,
    halo,
    hidden,
    leaving,
):
    first, last, spot = position()
    build_halo(near, far, halo)
    kernels = ((kernels0, 0), (kernels1, 32), (kernels2, 0), (kernels3, 0))
    build_first(spot, kernels, w1_full)
    w2_own[...] = jnp.concatenate(
        [
            jnp.concatenate(
                [
                    strip(kernels0, 0, 3 + 3 * (1 + q - z) + b)[:, 64 * c : 64 * c + 64]
                    for q in range(2)
                    for b in range(3)
                ],
                1,
            )
            for z in range(2)
            for c in range(3)
        ],
        0,
    )

    turned = jnp.concatenate(
        [
            jnp.concatenate([strip(*kernels[r], 3 + 3 * (1 + z - q) + b) for z in range(2)], 1)
            for b in range(3)
            for q in range(2)
            for r in range(4)
        ],
        0,
    )
    w2_turned[...] = turned.T.reshape(6, 64, 384)
    weights = w1_full[...].reshape(192, 192)
    copies = []
    for z in range(4):
        for base in range(-2, 10, 4):
            ys = range(base, base + 4)
            cells = jnp.concatenate([stacked_rows(vol, halo, z, y) for y in ys], 1)
            product = dot(weights, cells)
            for n, y in enumerate(ys):
                part = product[:, n * 128 : n * 128 + 128]
                pre = shifted(part[:64], 1) + part[64:128] + shifted(part[128:], -1)
                sigma = 1.0 / (1.0 + jnp.exp(-pre))
                value = pre * sigma
                steep = sigma * (1.0 + pre * (1.0 - sigma))
                if not 0 <= y < 8:
                    outside = first if y < 0 else last
                    value = jnp.where(outside, 0.0, value)
                    steep = jnp.where(outside, 0.0, steep)
                hidden[z, y + 2] = value.astype(BF)
                slope[z, y + 2] = steep
        copies.append(pltpu.make_async_copy(hidden.at[z], hidden_out.at[z], leaving.at[z]))
        copies[z].start()
    total = None
    for p in range(2):
        for base in range(0, 8, 4):
            ys = range(base, base + 4)
            left = []
            for y in ys:
                pieces = []
                for q in range(2):
                    own = part0[8 * (p + 2 * q) + y]
                    wide = own.astype(F32)
                    pieces += [shifted(wide, -2).astype(BF), own, shifted(wide, 2).astype(BF)]
                left.append(jnp.concatenate(pieces, 0))
            term = dot_cells(jnp.concatenate(left, 1), hidden_rows(hidden, p, ys))
            total = term if total is None else total + term
    grads[...] = total
    for copy in copies:
        copy.wait()


def hidden_rows(hidden, p, ys):
    return jnp.concatenate(
        [
            jnp.concatenate([hidden[p + 2 * q, y + 2 * b] for q in range(2) for b in range(3)], 0)
            for y in ys
        ],
        1,
    )


def grad_rows(parts, rims, p, ys, taps=range(3)):
    odd = lax.axis_index("z") & 1

    def grad_row(r, z, y):
        if 0 <= y < 8:
            return parts[r][8 * z + y]
        if rims is None:
            return jnp.zeros((16, 128), BF)
        return rims[r][12 * (1 - odd) + 3 * z + y + 3 if y < 0 else 12 * odd + 3 * z + y - 8]

    return jnp.concatenate(
        [
            jnp.concatenate(
                [
                    grad_row(r, p + 2 * q, y - 2 * (b - 1))
                    for b in taps
                    for q in range(2)
                    for r in range(4)
                ],
                0,
            )
            for y in ys
        ],
        1,
    )


def first_grad_kernel(
    vol, halo, part0, part1, part2, part3, slope, second, w2_turned, packed, own_grad, w2_mine
):
    parts = (part0, part1, part2, part3)
    mine = pl.multiple_of(position()[2] * 16, 16)
    w2_mine[...] = w2_turned[:, pl.ds(mine, 16), :].reshape(96, 384)
    for p in range(2):
        for ys in (range(-2, 0), range(4), range(4, 8), range(8, 10)):
            taps = range(3) if 0 <= ys[0] < 8 else range(0, 1) if ys[0] < 0 else range(2, 3)
            weights = w2_mine[:, 128 * taps[0] : 128 * (taps[-1] + 1)]
            product = dot(weights, grad_rows(parts, None, p, ys, taps))
            for n, y in enumerate(ys):
                part = product[:, n * 128 : n * 128 + 128]
                for q in range(2):
                    k = 48 * q
                    value = (
                        shifted(part[k : k + 16], -2)
                        + part[k + 16 : k + 32]
                        + shifted(part[k + 32 : k + 48], 2)
                    )
                    value = value * slope[p + 2 * q, y + 2, pl.ds(mine, 16), :]
                    own_grad[p + 2 * q, y + 2] = value.astype(BF)
    total = None
    for z in range(4):
        for base in range(-2, 10, 4):
            ys = range(base, base + 4)
            left = []
            for y in ys:
                own = own_grad[z, y + 2]
                wide = own.astype(F32)
                left.append(
                    jnp.concatenate([shifted(wide, -1).astype(BF), own, shifted(wide, 1).astype(BF)], 0)
                )
            source = jnp.concatenate([stacked_rows(vol, halo, z, y) for y in ys], 1)
            term = dot_cells(jnp.concatenate(left, 1), source)
            total = term if total is None else total + term
    raw = second[...]
    rows = jnp.concatenate(
        [raw[48:, :192], raw[:48, :192] + raw[48:, 192:], raw[:48, 192:], total], 0
    ) * (1.0 / 512.0)
    for k in range(24):
        packed[k] = rows[8 * k : 8 * k + 8, :128]
    for k in range(12):
        packed[24 + k] = jnp.concatenate(
            [rows[8 * k : 8 * k + 8, 128:], rows[96 + 8 * k : 104 + 8 * k, 128:]], 1
        )
    packed[36:] = jnp.zeros((28, 8, 128), F32)


def output_kernel(hidden, w2_own, out):
    weights = w2_own[...]
    for p in range(2):
        for base in range(0, 8, 4):
            ys = range(base, base + 4)
            product = dot(weights, hidden_rows(hidden, p, ys))
            for n, y in enumerate(ys):
                part = product[:, n * 128 : n * 128 + 128]
                for q in range(2):
                    k = 48 * q
                    value = (
                        shifted(part[k : k + 16], 2)
                        + part[k + 16 : k + 32]
                        + shifted(part[k + 32 : k + 48], -2)
                    )
                    out[p + 2 * q, y] = value.astype(BF)


def input_grad_kernel(
    part0,
    part1,
    part2,
    part3,
    rim0,
    rim1,
    rim2,
    rim3,
    slope,
    w1_full,
    w2_turned,
    input_grad,
    pre_grad,
    w1_turned,
):
    parts = (part0, part1, part2, part3)
    rims = (rim0, rim1, rim2, rim3)
    mine = pl.multiple_of(position()[2] * 16, 16)
    weights = w2_turned[...].reshape(384, 384)
    for p in range(2):
        for base in range(-1, 9, 2):
            ys = range(base, base + 2)
            product = dot(weights, grad_rows(parts, rims, p, ys))
            for n, y in enumerate(ys):
                part = product[:, n * 128 : n * 128 + 128]
                for q in range(2):
                    k = 192 * q
                    value = (
                        shifted(part[k : k + 64], -2)
                        + part[k + 64 : k + 128]
                        + shifted(part[k + 128 : k + 192], 2)
                    )
                    value = value * slope[p + 2 * q, y + 2]
                    pre_grad[p + 2 * q, y + 1] = value.astype(BF)
    for c in range(3):
        turned = w1_full[c].astype(F32).T
        w1_turned[c] = jnp.concatenate([turned[64 * b : 64 * b + 64] for b in range(3)], 1)
    weights = w1_turned[:, pl.ds(mine, 16), :].reshape(48, 192).astype(BF)
    for z in range(4):
        for base in range(0, 8, 4):
            ys = range(base, base + 4)
            cells = jnp.concatenate(
                [jnp.concatenate([pre_grad[z, y + 2 - b] for b in range(3)], 0) for y in ys], 1
            )
            product = dot(weights, cells)
            for n, y in enumerate(ys):
                part = product[:, n * 128 : n * 128 + 128]
                value = shifted(part[:16], -1) + part[16:32] + shifted(part[32:48], 1)
                input_grad[z, y] = value.astype(BF)


def sum_kernel(shares, summed):
    summed[...] = jnp.broadcast_to(jnp.sum(shares[...], 0).astype(BF)[None], (64, 8, 128))


def spread_kernel(tiles, first, second):
    for g in range(4):
        for c in range(3):
            for half in range(2):
                t = g * 6 + c * 2 + half
                main = tiles[t].astype(F32)
                rest = tiles[24 + t % 12].astype(F32)
                parts = [main[:, :64], main[:, 64:], rest[:, :64] if t < 12 else rest[:, 64:]]
                for b in range(3):
                    if g < 3:
                        second[g, b, c, 8 * half : 8 * half + 8, :] = parts[b]
                    else:
                        first[b, c, 8 * half : 8 * half + 8, :] = parts[b]


VMEM = pl.BlockSpec(memory_space=pltpu.VMEM)


def call(kernel, operands, outs, scratch=(), source=pltpu.VMEM, near=True, far=()):
    operands = list(operands)
    for n in range(len(operands)):
        space = pltpu.HBM if n in far else source
        operands[n] = pltpu.with_memory_space_constraint(operands[n], space)
    return pl.pallas_call(
        kernel,
        in_specs=[VMEM] * len(operands),
        out_specs=tuple(
            pl.BlockSpec(memory_space=out[2] if len(out) > 2 else pltpu.VMEM) for out in outs
        ),
        out_shape=tuple(
            (out[2] if len(out) > 2 else pltpu.VMEM)(*out[:2])
            if near
            else jax.ShapeDtypeStruct(*out[:2])
            for out in outs
        ),
        scratch_shapes=list(scratch),
        compiler_params=pltpu.CompilerParams(vmem_limit_bytes=16 << 20),
    )(*operands)


PAIRS = [(i, i ^ 1) for i in range(64)]
GAPS = [pair for i in range(1, 63, 2) for pair in ((i, i + 1), (i + 1, i))]
ACROSS = [(i, 3 - i) for i in range(4)]


def per_device(volume, w_first, w_second, cotangent):
    rows = ((32, 16, 128), BF)
    taps = ((18, 16, 128), BF)
    edge = ((60, 16, 128), BF)
    vol, near, far, part0, kernels0, own = call(
        prepare_kernel,
        (volume, cotangent, w_first, w_second),
        (((4, 8, 64, 128), BF), edge, edge, rows, taps, ((50, 16, 128), BF)),
        source=pltpu.HBM,
    )
    kernels2 = lax.ppermute(kernels0, ("x_lo", "x_hi"), ACROSS)
    part2 = lax.ppermute(part0, "x_hi", SWAP)
    near = lax.ppermute(near, BLOCKS, PAIRS)
    far = lax.ppermute(far, BLOCKS, GAPS)
    part1 = lax.ppermute(own, "core", SWAP)
    part3 = lax.ppermute(part2, "core", SWAP)
    kernels3 = lax.ppermute(kernels2, "core", SWAP)
    rim0 = jnp.concatenate([near[:12], far[:12]], 0)
    rim1 = lax.ppermute(rim0, "core", SWAP)
    rim2 = lax.ppermute(rim0, "x_hi", SWAP)
    rim3 = lax.ppermute(rim2, "core", SWAP)
    parts = (part0, part1, part2, part3)
    rims = (rim0, rim1, rim2, rim3)
    hidden, slope, second, w1_full, w2_own, w2_turned, halo = call(
        forward_kernel,
        (vol, near, far, part0, kernels0, part1, kernels2, kernels3),
        (
            ((4, 12, 64, 128), BF, pltpu.HBM),
            ((4, 12, 64, 128), F32),
            ((96, 384), F32),
            ((3, 64, 192), BF),
            ((96, 384), BF),
            ((6, 64, 384), BF),
            ((4, 6, 64, 128), BF),
        ),
        [pltpu.VMEM((4, 12, 64, 128), BF), pltpu.SemaphoreType.DMA((4,))],
    )
    (packed,) = call(
        first_grad_kernel,
        (vol, halo) + parts + (slope, second, w2_turned),
        (((64, 8, 128), F32),),
        [pltpu.VMEM((4, 12, 16, 128), BF), pltpu.VMEM((96, 384), BF)],
    )
    shares = lax.all_to_all(packed, BLOCKS, 0, 0)
    (output,) = call(output_kernel, (hidden, w2_own), (((4, 8, 16, 128), BF),), far=(0,))
    (input_grad,) = call(
        input_grad_kernel,
        parts + rims + (slope, w1_full, w2_turned),
        (((4, 8, 16, 128), BF),),
        [pltpu.VMEM((4, 10, 64, 128), BF), pltpu.VMEM((3, 64, 192), F32)],
    )
    (summed,) = call(sum_kernel, (shares,), (((64, 8, 128), BF),))
    tiles = lax.all_to_all(summed, BLOCKS, 0, 0)
    first_grad, second_grad = call(
        spread_kernel, (tiles,), (((3, 3, 16, 64), F32), ((3, 3, 3, 16, 64), F32)), near=False
    )
    return (output.transpose(2, 0, 1, 3), input_grad.transpose(2, 0, 1, 3), first_grad, second_grad)


def solution(mesh):
    fine = Mesh(mesh.devices.reshape(tuple(SPLIT.values())), tuple(SPLIT))
    return jax.shard_map(
        per_device,
        mesh=fine,
        in_specs=(
            P(None, None, BLOCKS, None),
            P(None, None, FILT, None),
            P(None, None, None, FILT, None),
            P(FILT, None, BLOCKS, None),
        ),
        out_specs=(
            P(FILT, None, BLOCKS, None),
            P(FILT, None, BLOCKS, None),
            P(None, None, FILT, None),
            P(None, None, None, FILT, None),
        ),
        check_vma=False,
    )
```

```python
import jax
import jax.numpy as jnp
from jax import lax
from jax.experimental import pallas as pl
from jax.experimental.pallas import tpu as pltpu
from jax.sharding import Mesh, PartitionSpec as P


BLOCKS = ("x_lo", "y", "z")
FILT = ("x_hi", "core")
SPLIT = {"x_lo": 2, "y": 4, "z": 8, "x_hi": 2, "core": 2}
BF = jnp.bfloat16
F32 = jnp.float32
SWAP = [(0, 1), (1, 0)]


def dot(left, right):
    return lax.dot_general(left, right, (((1,), (0,)), ((), ())), preferred_element_type=F32)


def dot_cells(left, right):
    return lax.dot_general(left, right, (((1,), (1,)), ((), ())), preferred_element_type=F32)


def shifted(value, amount):
    lane = lax.broadcasted_iota(jnp.int32, value.shape, 1)
    width = value.shape[1]
    moved = pltpu.roll(value, amount % width, 1)
    inside = lane >= amount if amount > 0 else lane < width + amount
    return jnp.where(inside, moved, 0.0)


def prepare_kernel(volume, cotangent, w_first, w_second, vol, near, far, grads, kernels, own):
    odd = lax.axis_index("z") & 1
    for z in range(4):
        rows = jnp.swapaxes(volume[:, z].astype(F32), 0, 1).astype(BF)
        vol[z] = rows
        mine = jnp.swapaxes(cotangent[:, z].astype(F32), 0, 1).astype(BF)
        grads[8 * z : 8 * z + 8] = mine
        own[8 * z : 8 * z + 8] = mine
        for n in range(3):
            k = 3 * z + n
            for edge, start in ((near, 5 * (1 - odd)), (far, 5 * odd)):
                edge[k] = grads[8 * z + start + n]
                edge[12 + 4 * k : 16 + 4 * k] = vol[z, start + n].reshape(4, 16, 128)
    strips = [w_first[b, c] for c in range(3) for b in range(3)]
    strips += [w_second[a, b, c] for a in range(3) for b in range(3) for c in range(3)]
    for n in range(18):
        pair = jnp.concatenate(strips[2 * n : 2 * n + 2], 1)
        kernels[n] = pair
        own[32 + n] = pair


def position():
    block = lax.axis_index(BLOCKS)
    return block == 0, block == 63, lax.axis_index(FILT)


def strip(kernels, base, n):
    k = base + 3 * (n // 2)
    if n % 2 == 0:
        return jnp.concatenate([kernels[k], kernels[k + 1][:, :64]], 1)
    return jnp.concatenate([kernels[k + 1][:, 64:], kernels[k + 2]], 1)


def volume_row(vol, halo, z, y):
    if 0 <= y < 8:
        return vol[z, y]
    return halo[z, y + 3 if y < 0 else y - 5]


def stacked_rows(vol, halo, z, y):
    return jnp.concatenate([volume_row(vol, halo, z, y + n) for n in (-1, 0, 1)], 0)


def build_halo(near, far, halo):
    odd = lax.axis_index("z") & 1
    for edge, start in ((near, 3 * (1 - odd)), (far, 3 * odd)):
        for z in range(4):
            for n in range(3):
                k = 12 + 4 * (3 * z + n)
                halo[z, start + n] = edge[k : k + 4].reshape(64, 128)


def build_first(spot, kernels, w1_full):
    for r in range(4):
        f = pl.multiple_of((spot ^ r) * 16, 16)
        for c in range(3):
            w1_full[c, pl.ds(f, 16), :] = strip(*kernels[r], c)


def forward_kernel(
    vol,
    near,
    far,
    part0,
    kernels0,
    kernels1,
    kernels2,
    kernels3,
    hidden_out,
    slope,
    grads,
    w1_full,
    w2_own,
    w2_turned,
    halo,
    hidden,
    leaving,
):
    first, last, spot = position()
    build_halo(near, far, halo)
    kernels = ((kernels0, 0), (kernels1, 32), (kernels2, 0), (kernels3, 0))
    build_first(spot, kernels, w1_full)
    w2_own[...] = jnp.concatenate(
        [
            jnp.concatenate(
                [
                    strip(kernels0, 0, 3 + 3 * (1 + q - z) + b)[:, 64 * c : 64 * c + 64]
                    for q in range(2)
                    for b in range(3)
                ],
                1,
            )
            for z in range(2)
            for c in range(3)
        ],
        0,
    )

    turned = jnp.concatenate(
        [
            jnp.concatenate([strip(*kernels[r], 3 + 3 * (1 + z - q) + b) for z in range(2)], 1)
            for b in range(3)
            for q in range(2)
            for r in range(4)
        ],
        0,
    )
    w2_turned[...] = turned.T.reshape(6, 64, 384)
    weights = w1_full[...].reshape(192, 192)
    copies = []
    for z in range(4):
        for base in range(-2, 10, 4):
            ys = range(base, base + 4)
            cells = jnp.concatenate([stacked_rows(vol, halo, z, y) for y in ys], 1)
            product = dot(weights, cells)
            for n, y in enumerate(ys):
                part = product[:, n * 128 : n * 128 + 128]
                pre = shifted(part[:64], 1) + part[64:128] + shifted(part[128:], -1)
                sigma = 1.0 / (1.0 + jnp.exp(-pre))
                value = pre * sigma
                steep = sigma * (1.0 + pre * (1.0 - sigma))
                if not 0 <= y < 8:
                    outside = first if y < 0 else last
                    value = jnp.where(outside, 0.0, value)
                    steep = jnp.where(outside, 0.0, steep)
                hidden[z, y + 2] = value.astype(BF)
                slope[z, y + 2] = steep
        copies.append(pltpu.make_async_copy(hidden.at[z], hidden_out.at[z], leaving.at[z]))
        copies[z].start()
    total = None
    for p in range(2):
        for base in range(0, 8, 4):
            ys = range(base, base + 4)
            left = []
            for y in ys:
                pieces = []
                for q in range(2):
                    own = part0[8 * (p + 2 * q) + y]
                    wide = own.astype(F32)
                    pieces += [shifted(wide, -2).astype(BF), own, shifted(wide, 2).astype(BF)]
                left.append(jnp.concatenate(pieces, 0))
            term = dot_cells(jnp.concatenate(left, 1), hidden_rows(hidden, p, ys))
            total = term if total is None else total + term
    grads[...] = total
    for copy in copies:
        copy.wait()


def hidden_rows(hidden, p, ys):
    return jnp.concatenate(
        [
            jnp.concatenate([hidden[p + 2 * q, y + 2 * b] for q in range(2) for b in range(3)], 0)
            for y in ys
        ],
        1,
    )


def grad_rows(parts, rims, p, ys, taps=range(3)):
    odd = lax.axis_index("z") & 1

    def grad_row(r, z, y):
        if 0 <= y < 8:
            return parts[r][8 * z + y]
        if rims is None:
            return jnp.zeros((16, 128), BF)
        return rims[r][12 * (1 - odd) + 3 * z + y + 3 if y < 0 else 12 * odd + 3 * z + y - 8]

    return jnp.concatenate(
        [
            jnp.concatenate(
                [
                    grad_row(r, p + 2 * q, y - 2 * (b - 1))
                    for b in taps
                    for q in range(2)
                    for r in range(4)
                ],
                0,
            )
            for y in ys
        ],
        1,
    )


def first_grad_kernel(
    vol, halo, part0, part1, part2, part3, slope, second, w2_turned, packed, own_grad, w2_mine
):
    parts = (part0, part1, part2, part3)
    mine = pl.multiple_of(position()[2] * 16, 16)
    w2_mine[...] = w2_turned[:, pl.ds(mine, 16), :].reshape(96, 384)
    for p in range(2):
        for ys in (range(-2, 0), range(4), range(4, 8), range(8, 10)):
            taps = range(3) if 0 <= ys[0] < 8 else range(0, 1) if ys[0] < 0 else range(2, 3)
            weights = w2_mine[:, 128 * taps[0] : 128 * (taps[-1] + 1)]
            product = dot(weights, grad_rows(parts, None, p, ys, taps))
            for n, y in enumerate(ys):
                part = product[:, n * 128 : n * 128 + 128]
                for q in range(2):
                    k = 48 * q
                    value = (
                        shifted(part[k : k + 16], -2)
                        + part[k + 16 : k + 32]
                        + shifted(part[k + 32 : k + 48], 2)
                    )
                    value = value * slope[p + 2 * q, y + 2, pl.ds(mine, 16), :]
                    own_grad[p + 2 * q, y + 2] = value.astype(BF)
    total = None
    for z in range(4):
        for base in range(-2, 10, 4):
            ys = range(base, base + 4)
            left = []
            for y in ys:
                own = own_grad[z, y + 2]
                wide = own.astype(F32)
                left.append(
                    jnp.concatenate([shifted(wide, -1).astype(BF), own, shifted(wide, 1).astype(BF)], 0)
                )
            source = jnp.concatenate([stacked_rows(vol, halo, z, y) for y in ys], 1)
            term = dot_cells(jnp.concatenate(left, 1), source)
            total = term if total is None else total + term
    raw = second[...]
    rows = jnp.concatenate(
        [raw[48:, :192], raw[:48, :192] + raw[48:, 192:], raw[:48, 192:], total], 0
    ) * (1.0 / 512.0)
    rows = rows.astype(BF)
    for k in range(24):
        packed[k] = rows[8 * k : 8 * k + 8, :128]
    for k in range(12):
        packed[24 + k] = jnp.concatenate(
            [rows[8 * k : 8 * k + 8, 128:], rows[96 + 8 * k : 104 + 8 * k, 128:]], 1
        )
    packed[36:] = jnp.zeros((28, 8, 128), BF)


def output_kernel(hidden, w2_own, out):
    weights = w2_own[...]
    for p in range(2):
        for base in range(0, 8, 4):
            ys = range(base, base + 4)
            product = dot(weights, hidden_rows(hidden, p, ys))
            for n, y in enumerate(ys):
                part = product[:, n * 128 : n * 128 + 128]
                for q in range(2):
                    k = 48 * q
                    value = (
                        shifted(part[k : k + 16], 2)
                        + part[k + 16 : k + 32]
                        + shifted(part[k + 32 : k + 48], -2)
                    )
                    out[p + 2 * q, y] = value.astype(BF)


def input_grad_kernel(
    part0,
    part1,
    part2,
    part3,
    rim0,
    rim1,
    rim2,
    rim3,
    slope,
    w1_full,
    w2_turned,
    input_grad,
    pre_grad,
    w1_turned,
):
    parts = (part0, part1, part2, part3)
    rims = (rim0, rim1, rim2, rim3)
    mine = pl.multiple_of(position()[2] * 16, 16)
    weights = w2_turned[...].reshape(384, 384)
    for p in range(2):
        for base in range(-1, 9, 2):
            ys = range(base, base + 2)
            product = dot(weights, grad_rows(parts, rims, p, ys))
            for n, y in enumerate(ys):
                part = product[:, n * 128 : n * 128 + 128]
                for q in range(2):
                    k = 192 * q
                    value = (
                        shifted(part[k : k + 64], -2)
                        + part[k + 64 : k + 128]
                        + shifted(part[k + 128 : k + 192], 2)
                    )
                    value = value * slope[p + 2 * q, y + 2]
                    pre_grad[p + 2 * q, y + 1] = value.astype(BF)
    for c in range(3):
        turned = w1_full[c].astype(F32).T
        w1_turned[c] = jnp.concatenate([turned[64 * b : 64 * b + 64] for b in range(3)], 1)
    weights = w1_turned[:, pl.ds(mine, 16), :].reshape(48, 192).astype(BF)
    for z in range(4):
        for base in range(0, 8, 4):
            ys = range(base, base + 4)
            cells = jnp.concatenate(
                [jnp.concatenate([pre_grad[z, y + 2 - b] for b in range(3)], 0) for y in ys], 1
            )
            product = dot(weights, cells)
            for n, y in enumerate(ys):
                part = product[:, n * 128 : n * 128 + 128]
                value = shifted(part[:16], -1) + part[16:32] + shifted(part[32:48], 1)
                input_grad[z, y] = value.astype(BF)


def sum_kernel(shares, summed):
    summed[...] = jnp.broadcast_to(jnp.sum(shares[...].astype(F32), 0).astype(BF)[None], (64, 8, 128))


def spread_kernel(tiles, first, second):
    for g in range(4):
        for c in range(3):
            for half in range(2):
                t = g * 6 + c * 2 + half
                main = tiles[t].astype(F32)
                rest = tiles[24 + t % 12].astype(F32)
                parts = [main[:, :64], main[:, 64:], rest[:, :64] if t < 12 else rest[:, 64:]]
                for b in range(3):
                    if g < 3:
                        second[g, b, c, 8 * half : 8 * half + 8, :] = parts[b]
                    else:
                        first[b, c, 8 * half : 8 * half + 8, :] = parts[b]


VMEM = pl.BlockSpec(memory_space=pltpu.VMEM)


def call(kernel, operands, outs, scratch=(), source=pltpu.VMEM, near=True, far=()):
    operands = list(operands)
    for n in range(len(operands)):
        space = pltpu.HBM if n in far else source
        operands[n] = pltpu.with_memory_space_constraint(operands[n], space)
    return pl.pallas_call(
        kernel,
        in_specs=[VMEM] * len(operands),
        out_specs=tuple(
            pl.BlockSpec(memory_space=out[2] if len(out) > 2 else pltpu.VMEM) for out in outs
        ),
        out_shape=tuple(
            (out[2] if len(out) > 2 else pltpu.VMEM)(*out[:2])
            if near
            else jax.ShapeDtypeStruct(*out[:2])
            for out in outs
        ),
        scratch_shapes=list(scratch),
        compiler_params=pltpu.CompilerParams(vmem_limit_bytes=16 << 20),
    )(*operands)


PAIRS = [(i, i ^ 1) for i in range(64)]
GAPS = [pair for i in range(1, 63, 2) for pair in ((i, i + 1), (i + 1, i))]
ACROSS = [(i, 3 - i) for i in range(4)]


def per_device(volume, w_first, w_second, cotangent):
    rows = ((32, 16, 128), BF)
    taps = ((18, 16, 128), BF)
    edge = ((60, 16, 128), BF)
    vol, near, far, part0, kernels0, own = call(
        prepare_kernel,
        (volume, cotangent, w_first, w_second),
        (((4, 8, 64, 128), BF), edge, edge, rows, taps, ((50, 16, 128), BF)),
        source=pltpu.HBM,
    )
    kernels2 = lax.ppermute(kernels0, ("x_lo", "x_hi"), ACROSS)
    part2 = lax.ppermute(part0, "x_hi", SWAP)
    near = lax.ppermute(near, BLOCKS, PAIRS)
    far = lax.ppermute(far, BLOCKS, GAPS)
    part1 = lax.ppermute(own, "core", SWAP)
    part3 = lax.ppermute(part2, "core", SWAP)
    kernels3 = lax.ppermute(kernels2, "core", SWAP)
    rim0 = jnp.concatenate([near[:12], far[:12]], 0)
    rim1 = lax.ppermute(rim0, "core", SWAP)
    rim2 = lax.ppermute(rim0, "x_hi", SWAP)
    rim3 = lax.ppermute(rim2, "core", SWAP)
    parts = (part0, part1, part2, part3)
    rims = (rim0, rim1, rim2, rim3)
    hidden, slope, second, w1_full, w2_own, w2_turned, halo = call(
        forward_kernel,
        (vol, near, far, part0, kernels0, part1, kernels2, kernels3),
        (
            ((4, 12, 64, 128), BF, pltpu.HBM),
            ((4, 12, 64, 128), F32),
            ((96, 384), F32),
            ((3, 64, 192), BF),
            ((96, 384), BF),
            ((6, 64, 384), BF),
            ((4, 6, 64, 128), BF),
        ),
        [pltpu.VMEM((4, 12, 64, 128), BF), pltpu.SemaphoreType.DMA((4,))],
    )
    (packed,) = call(
        first_grad_kernel,
        (vol, halo) + parts + (slope, second, w2_turned),
        (((64, 8, 128), BF),),
        [pltpu.VMEM((4, 12, 16, 128), BF), pltpu.VMEM((96, 384), BF)],
    )
    shares = lax.all_to_all(packed, BLOCKS, 0, 0)
    (output,) = call(output_kernel, (hidden, w2_own), (((4, 8, 16, 128), BF),), far=(0,))
    (input_grad,) = call(
        input_grad_kernel,
        parts + rims + (slope, w1_full, w2_turned),
        (((4, 8, 16, 128), BF),),
        [pltpu.VMEM((4, 10, 64, 128), BF), pltpu.VMEM((3, 64, 192), F32)],
    )
    (summed,) = call(sum_kernel, (shares,), (((64, 8, 128), BF),))
    tiles = lax.all_to_all(summed, BLOCKS, 0, 0)
    first_grad, second_grad = call(
        spread_kernel, (tiles,), (((3, 3, 16, 64), F32), ((3, 3, 3, 16, 64), F32)), near=False
    )
    return (output.transpose(2, 0, 1, 3), input_grad.transpose(2, 0, 1, 3), first_grad, second_grad)


def solution(mesh):
    fine = Mesh(mesh.devices.reshape(tuple(SPLIT.values())), tuple(SPLIT))
    return jax.shard_map(
        per_device,
        mesh=fine,
        in_specs=(
            P(None, None, BLOCKS, None),
            P(None, None, FILT, None),
            P(None, None, None, FILT, None),
            P(FILT, None, BLOCKS, None),
        ),
        out_specs=(
            P(FILT, None, BLOCKS, None),
            P(FILT, None, BLOCKS, None),
            P(None, None, FILT, None),
            P(None, None, None, FILT, None),
        ),
        check_vma=False,
    )
```
